32 devices in a mesh: blk: 16 (over z, x, core), grp: 2 (over y).
Axes of the slice: x: 2, y: 2, z: 4, core: 2. Of those that a mesh axis runs over, the one named last changes fastest.
Arguments:
- amplitudes: bfloat16 [16, 2, 16, 3, 128, 128], P('blk', 'grp'), may hold values from -6 to 6
- integral_slabs: bfloat16 [2, 2048, 512], P('grp', 'blk'), may hold values from -0.125 to 0.125
- tile_tasks: int32 [16, 2, 16, 3], P('blk', 'grp'), may hold values from -1 to 47, as said below
- owner_map: int32 [48], replicated, may hold values from 0 to 47, as said below
Outputs:
- residual: float32 [6144, 512], P('blk', 'grp')
The draws below stay inside these ranges and needn't reach their ends.
Inputs may be any that keep to these rules, and one draw needn't show every extreme that they name: For a live entry I = tile_tasks[b, g, s, m], owner_map[I] // 3 == b; the live entries of one [b, g, s] are distinct and occupy its first slots; every [b, g] has at least one slab whose 3 slots are all live. `owner_map`: A permutation of the ij tiles.
All inputs are finite; a program needn't handle non-finite values.
Results may differ from the reference program's by a relative error of at most 0.0003.
Values may be sent and summed in bfloat16 or wider, within the bound.
A program may use at most 128 MiB of HBM per device.

```python
import jax
import jax.numpy as jnp
from jax import lax

OT = 128
VT = 128
MOST = 3
HOLD = 3
AB = 512
SLABS = 16
GROUPS = 2
NIT = 48


def owner_permutation(key):
    return jax.random.permutation(jax.random.fold_in(key, 11), NIT).astype(jnp.int32)


def draw_owner_map(key, part):
    return owner_permutation(key)


def draw_tile_tasks(key, part):
    owners = owner_permutation(key)
    inverse = jnp.zeros((NIT,), jnp.int32).at[owners].set(jnp.arange(NIT, dtype=jnp.int32))
    key_level, key_drop, key_full, key_order = jax.random.split(jax.random.fold_in(key, 23), 4)
    busy_level = jax.random.randint(key_level, (SLABS, GROUPS, 1), 1, MOST + 1)
    dropped = jax.random.randint(key_drop, (SLABS, GROUPS, SLABS), 0, 2)
    live_count = jnp.clip(busy_level - dropped, 0, MOST)
    full_slab = jax.random.randint(key_full, (SLABS, GROUPS, 1), 0, SLABS)
    slab_iota = jnp.arange(SLABS, dtype=jnp.int32)[None, None, :]
    live_count = jnp.where(slab_iota == full_slab, MOST, live_count)
    scores = jax.random.randint(key_order, (SLABS, GROUPS, SLABS, HOLD), 0, 4096) * HOLD
    scores = scores + jnp.arange(HOLD, dtype=jnp.int32)
    row_order = jnp.argsort(scores, axis=-1)[..., :MOST].astype(jnp.int32)
    holder = jnp.arange(SLABS, dtype=jnp.int32)[:, None, None, None]
    slot_index = holder * HOLD + row_order
    tile_ids = inverse[slot_index]
    live_slot = jnp.arange(MOST, dtype=jnp.int32)[None, None, None, :] < live_count[..., None]
    return jnp.where(live_slot, tile_ids, -1).astype(jnp.int32)


def levels(key, shape, cuts, smallest, high):
    def one(position, parts):
        draws = jax.random.uniform(jax.random.fold_in(jax.random.fold_in(key, 6), position), (parts,), jnp.float32, smallest / len(cuts), high / len(cuts))
        return jnp.repeat(jnp.exp(draws), shape[position] // parts).reshape((-1,) + (1,) * (len(shape) - position - 1))

    level = one(*cuts[0])
    for cut in cuts[1:]:
        level = level * one(*cut)
    return level


def bell_draw(own_key, shape, deviation, reach, shards=(), kind=jnp.bfloat16):
    array = jax.random.normal(own_key, shape, jnp.float32) * deviation
    if len(shards) > 0:
        array = levels(own_key, shape, shards, -0.22, 0.18) * array
    return jnp.clip(array, min=-reach, max=reach).astype(kind)


def setup_inputs(seed: int = 0) -> dict:
    seeds = jax.random.split(jax.random.key(seed), 5)
    amplitudes = bell_draw(seeds[0], (SLABS, GROUPS, SLABS, MOST, OT, VT), 1.0, 6.0, ((0, 16), (1, 2)))
    integral_slabs = bell_draw(seeds[1], (GROUPS, SLABS * VT, AB), (GROUPS * SLABS * VT // 2) ** -0.5, 0.125, ((0, 2), (1, 16)))
    tile_tasks = draw_tile_tasks(jax.random.fold_in(seeds[4], 71), 0)
    owner_map = draw_owner_map(jax.random.fold_in(seeds[4], 71), 0)
    return {"amplitudes": amplitudes, "integral_slabs": integral_slabs, "tile_tasks": tile_tasks, "owner_map": owner_map}


def reference(amplitudes, integral_slabs, tile_tasks, owner_map):
    totals = jnp.zeros((NIT + 1, OT, AB), jnp.float32)
    for group in range(GROUPS):
        group_tiles = amplitudes[:, group]
        group_tasks = tile_tasks[:, group]
        group_slab = integral_slabs[group]

        def slab_step(totals, slab_num):
            tiles_now = lax.dynamic_index_in_dim(group_tiles, slab_num, 1, keepdims=False)
            slab_rows = lax.dynamic_slice_in_dim(group_slab, slab_num * VT, VT, 0)
            product = jnp.dot(tiles_now.reshape(-1, VT), slab_rows, preferred_element_type=jnp.float32)
            product = product.reshape(-1, OT, AB)
            targets = lax.dynamic_index_in_dim(group_tasks, slab_num, 1, keepdims=False).reshape(-1)
            targets = jnp.where(targets >= 0, targets, NIT).astype(jnp.int32)
            return totals.at[targets].add(product), None

        totals, _ = lax.scan(slab_step, totals, jnp.arange(SLABS, dtype=jnp.int32))
    ordered = jnp.zeros((NIT, OT, AB), jnp.float32).at[owner_map].set(totals[:NIT])
    return ordered.reshape(NIT * OT, AB)
```

```python
import functools

import jax
import jax.numpy as jnp
from jax import lax
from jax.experimental import pallas as pl
from jax.experimental.pallas import tpu as pltpu
from jax.sharding import PartitionSpec as P

MESH = pl.DeviceIdType.MESH
LANES = 128
ROW = 2
CORES = 2


def for_range(low, high, body):
    if high - low <= 8:
        for i in range(low, high):
            body(i)
    else:
        pl.loop(low, high)(body)


def kernel(
    dims,
    tasks_ref,
    owner_ref,
    amp_hbm,
    slab_hbm,
    keep_ref,
    recv_ref,
    amp_ref,
    slabs,
    dense,
    outgoing,
    amp_sem,
    slab_sem,
    line_send,
    line_recv,
    row_send,
    row_recv,
    core_send,
    core_recv,
    sum_send,
    sum_recv,
):
    lines, hold, most, rows, depth, half = dims
    chunks = half // LANES
    steps = 2 * chunks
    me = lax.axis_index("blk")
    grp = lax.axis_index("grp")
    core = me % CORES
    row = (me // CORES) % ROW
    line = me // (CORES * ROW)

    def blk_of(z, x, c):
        return (z * ROW + x) * CORES + c

    def line_peer(i):
        return blk_of((line + i) % lines, row, core)

    row_peer = blk_of(line, 1 - row, core)
    core_peer = blk_of(line, row, 1 - core)

    def column(k):
        side = 1 - grp if k < chunks else grp
        return pl.multiple_of(side * half + (k % chunks) * LANES, LANES)

    loads = [
        pltpu.make_async_copy(
            slab_hbm.at[:, pl.ds(column(k), LANES)], slabs.at[k, 0, 0, 0], slab_sem.at[k]
        )
        for k in range(steps)
    ]
    for load in loads:
        load.start()
    amp_load = pltpu.make_async_copy(amp_hbm, amp_ref, amp_sem)
    amp_load.start()

    barrier = pltpu.get_barrier_semaphore()

    def greet(blk, g):
        pl.semaphore_signal(barrier, inc=1, device_id=(blk, g), device_id_type=MESH)

    for_range(1, lines, lambda i: greet(line_peer(i), grp))
    greet(row_peer, grp)
    greet(core_peer, grp)
    greet(me, 1 - grp)

    def line_copy(k, i):
        return pltpu.make_async_remote_copy(
            src_ref=slabs.at[k, 0, 0, 0],
            dst_ref=slabs.at[k, 0, i, 0],
            send_sem=line_send.at[k, i],
            recv_sem=line_recv.at[k, i],
            device_id=(line_peer(lines - i), grp),
            device_id_type=MESH,
        )

    def row_copy(k, i):
        return pltpu.make_async_remote_copy(
            src_ref=slabs.at[k, 0, i, 0],
            dst_ref=slabs.at[k, 1, i, 0],
            send_sem=row_send.at[k, i],
            recv_sem=row_recv.at[k, i],
            device_id=(row_peer, grp),
            device_id_type=MESH,
        )

    def core_copy(k, x, i):
        return pltpu.make_async_remote_copy(
            src_ref=slabs.at[k, x, i, 0],
            dst_ref=slabs.at[k, x, i, 1],
            send_sem=core_send.at[k, x, i],
            recv_sem=core_recv.at[k, x, i],
            device_id=(core_peer, grp),
            device_id_type=MESH,
        )

    def sum_copy(k, h):
        at = pl.ds(h * rows, rows)
        return pltpu.make_async_remote_copy(
            src_ref=outgoing.at[k, at],
            dst_ref=recv_ref.at[at, pl.ds(k * LANES, LANES)],
            send_sem=sum_send.at[k, h],
            recv_sem=sum_recv.at[k, h],
            device_id=(me, 1 - grp),
            device_id_type=MESH,
        )

    def line_sends(k):
        loads[k].wait()
        for_range(1, lines, lambda i: line_copy(k, i).start())

    def own_sends(k):
        row_copy(k, 0).start()
        core_copy(k, 0, 0).start()

    def line_arrivals(k):
        def arrive(i):
            line_copy(k, i).wait_recv()
            row_copy(k, i).start()
            core_copy(k, 0, i).start()

        for_range(1, lines, arrive)

    def row_arrivals(k):
        def arrive(i):
            row_copy(k, i).wait_recv()
            core_copy(k, 1, i).start()

        for_range(0, lines, arrive)

    def core_arrivals(k, x):
        for_range(0, lines, lambda i: core_copy(k, x, i).wait_recv())

    pl.semaphore_wait(barrier, lines + 2)
    for k in range(steps):
        line_sends(k)
        if k < 2:
            own_sends(k)

    amp_load.wait()
    for x in range(ROW):
        for c in range(CORES):

            def fill(i, x=x, c=c):
                source = blk_of(
                    (line + i) % lines,
                    (row + x) % ROW,
                    (core + c) % CORES,
                )
                tiles = []
                for m in range(most):
                    task = tasks_ref[m, 0, source]
                    local = owner_ref[jnp.maximum(task, 0)] - me * hold
                    tiles.append(jnp.where(task >= 0, local, -1))
                at = pl.multiple_of(((x * lines + i) * CORES + c) * depth, depth)
                for h in range(hold):
                    slot = jnp.int32(0)
                    live = jnp.int32(0)
                    for m in range(most):
                        hit = tiles[m] == h
                        slot = jnp.where(hit, m, slot)
                        live = jnp.where(hit, 1, live)
                    tile = amp_ref[source, slot]
                    dense[h * rows : (h + 1) * rows, pl.ds(at, depth)] = jnp.where(
                        live > 0, tile, jnp.zeros_like(tile)
                    )

            for_range(0, lines, fill)

    span = lines * CORES * depth

    def product(k, x):
        width = min(span, 2048)

        def term(j):
            first = pl.multiple_of(j * width, width)
            block = slabs[k, x, pl.ds(j * (width // (CORES * depth)), width // (CORES * depth))]
            return jnp.dot(
                dense[:, pl.ds(x * span + first, width)],
                block.reshape(width, LANES),
                preferred_element_type=jnp.float32,
            )

        if span == width:
            return term(0)
        zero = jnp.zeros((hold * rows, LANES), jnp.float32)
        return lax.fori_loop(0, span // width, lambda j, total: total + term(j), zero)

    def near(k):
        core_arrivals(k, 0)
        if k < chunks:
            outgoing[k] = product(k, 0)
        else:
            keep_ref[:, pl.ds((k - chunks) * LANES, LANES)] = product(k, 0)

    def far(k):
        core_arrivals(k, 1)
        if k < chunks:
            outgoing[k] += product(k, 1)
            for h in range(hold):
                sum_copy(k, h).start()
        else:
            keep_ref[:, pl.ds((k - chunks) * LANES, LANES)] += product(k, 1)

    line_arrivals(0)
    for k in range(steps):
        if k + 2 < steps:
            own_sends(k + 2)
        if k + 1 < steps:
            line_arrivals(k + 1)
        row_arrivals(k)
        near(k)
        far(k)

    for k in range(chunks):
        for h in range(hold):
            sum_copy(k, h).wait()
    for k in range(steps):
        for_range(1, lines, lambda i: line_copy(k, i).wait_send())

        def sent(i):
            row_copy(k, i).wait_send()
            for x in range(ROW):
                core_copy(k, x, i).wait_send()

        for_range(0, lines, sent)


def per_device(mesh, amplitudes, integral_slabs, tile_tasks, owner_map):
    amp = amplitudes[0, 0]
    slab = integral_slabs[0]
    count, most, rows, depth = amp.shape
    devices, groups = mesh.shape["blk"], mesh.shape["grp"]
    hold = owner_map.shape[0] // devices
    columns = slab.shape[1]
    half = columns // groups
    lines = devices // (ROW * CORES)
    chunks = half // LANES
    steps = groups * chunks
    dma = pltpu.SemaphoreType.DMA
    total = jax.ShapeDtypeStruct((hold * rows, half), jnp.float32)
    keep, recv = pl.pallas_call(
        functools.partial(kernel, (lines, hold, most, rows, depth, half)),
        out_shape=(total, total),
        in_specs=[
            pl.BlockSpec(memory_space=pltpu.SMEM),
            pl.BlockSpec(memory_space=pltpu.SMEM),
            pl.BlockSpec(memory_space=pl.ANY),
            pl.BlockSpec(memory_space=pl.ANY),
        ],
        out_specs=(
            pl.BlockSpec(memory_space=pltpu.VMEM),
            pl.BlockSpec(memory_space=pltpu.VMEM),
        ),
        scratch_shapes=[
            pltpu.VMEM(amp.shape, amp.dtype),
            pltpu.VMEM((steps, ROW, lines, CORES, depth, LANES), slab.dtype),
            pltpu.VMEM((hold * rows, count * depth), amp.dtype),
            pltpu.VMEM((chunks, hold * rows, LANES), jnp.float32),
            dma,
            dma((steps,)),
            dma((steps, lines)),
            dma((steps, lines)),
            dma((steps, lines)),
            dma((steps, lines)),
            dma((steps, ROW, lines)),
            dma((steps, ROW, lines)),
            dma((chunks, hold)),
            dma((chunks, hold)),
        ],
        compiler_params=pltpu.CompilerParams(
            collective_id=0, has_side_effects=True, vmem_limit_bytes=60 * 1024 * 1024
        ),
    )(tile_tasks[0].transpose(2, 0, 1), owner_map, amp, slab)
    return keep + recv


def solution(mesh):
    placed = (
        P("blk", "grp", None, None, None, None),
        P("grp", "blk", None),
        P("blk", "grp", None, None),
        P(),
    )
    return jax.shard_map(
        functools.partial(per_device, mesh),
        mesh=mesh,
        in_specs=placed,
        out_specs=P("blk", "grp"),
        check_vma=False,
    )
```

```python
import functools

import jax
import jax.numpy as jnp
from jax import lax
from jax.experimental import pallas as pl
from jax.experimental.pallas import tpu as pltpu
from jax.sharding import PartitionSpec as P

MESH = pl.DeviceIdType.MESH
LANES = 128
ROW = 2
CORES = 2


def for_range(low, high, body):
    if high - low <= 8:
        for i in range(low, high):
            body(i)
    else:
        pl.loop(low, high)(body)


def kernel(
    dims,
    tasks_ref,
    owner_ref,
    amp_hbm,
    slab_hbm,
    keep_ref,
    recv_ref,
    amp_ref,
    slabs,
    dense,
    outgoing,
    amp_sem,
    slab_sem,
    line_send,
    line_recv,
    row_send,
    row_recv,
    core_send,
    core_recv,
    sum_send,
    sum_recv,
):
    lines, hold, most, rows, depth, half = dims
    chunks = half // LANES
    steps = 2 * chunks
    me = lax.axis_index("blk")
    grp = lax.axis_index("grp")
    core = me % CORES
    row = (me // CORES) % ROW
    line = me // (CORES * ROW)

    def blk_of(z, x, c):
        return (z * ROW + x) * CORES + c

    def line_peer(i):
        return blk_of((line + i) % lines, row, core)

    row_peer = blk_of(line, 1 - row, core)
    core_peer = blk_of(line, row, 1 - core)

    def column(k):
        side = 1 - grp if k < chunks else grp
        return pl.multiple_of(side * half + (k % chunks) * LANES, LANES)

    loads = [
        pltpu.make_async_copy(
            slab_hbm.at[:, pl.ds(column(k), LANES)], slabs.at[k, 0, 0, 0], slab_sem.at[k]
        )
        for k in range(steps)
    ]
    for load in loads:
        load.start()
    amp_load = pltpu.make_async_copy(amp_hbm, amp_ref, amp_sem)
    amp_load.start()

    barrier = pltpu.get_barrier_semaphore()

    def greet(blk, g):
        pl.semaphore_signal(barrier, inc=1, device_id=(blk, g), device_id_type=MESH)

    for_range(1, lines, lambda i: greet(line_peer(i), grp))
    greet(row_peer, grp)
    greet(core_peer, grp)
    greet(me, 1 - grp)

    def line_copy(k, i):
        return pltpu.make_async_remote_copy(
            src_ref=slabs.at[k, 0, 0, 0],
            dst_ref=slabs.at[k, 0, i, 0],
            send_sem=line_send.at[k, i],
            recv_sem=line_recv.at[k, i],
            device_id=(line_peer(lines - i), grp),
            device_id_type=MESH,
        )

    def row_copy(k, i):
        return pltpu.make_async_remote_copy(
            src_ref=slabs.at[k, 0, i, 0],
            dst_ref=slabs.at[k, 1, i, 0],
            send_sem=row_send.at[k, i],
            recv_sem=row_recv.at[k, i],
            device_id=(row_peer, grp),
            device_id_type=MESH,
        )

    def core_copy(k, x, i):
        return pltpu.make_async_remote_copy(
            src_ref=slabs.at[k, x, i, 0],
            dst_ref=slabs.at[k, x, i, 1],
            send_sem=core_send.at[k, x, i],
            recv_sem=core_recv.at[k, x, i],
            device_id=(core_peer, grp),
            device_id_type=MESH,
        )

    def sum_copy(k, h):
        at = pl.ds(h * rows, rows)
        return pltpu.make_async_remote_copy(
            src_ref=outgoing.at[k, at],
            dst_ref=recv_ref.at[at, pl.ds(k * LANES, LANES)],
            send_sem=sum_send.at[k, h],
            recv_sem=sum_recv.at[k, h],
            device_id=(me, 1 - grp),
            device_id_type=MESH,
        )

    def line_sends(k):
        loads[k].wait()
        for_range(1, lines, lambda i: line_copy(k, lines - i).start())

    def own_sends(k):
        row_copy(k, 0).start()
        core_copy(k, 0, 0).start()

    def line_arrive(k, i):
        line_copy(k, i).wait_recv()
        row_copy(k, i).start()
        core_copy(k, 0, i).start()

    def row_arrive(k, i):
        row_copy(k, i).wait_recv()
        core_copy(k, 1, i).start()

    def line_arrivals(k):
        for_range(1, lines, lambda i: line_arrive(k, i))

    def row_arrivals(k):
        for_range(0, lines, lambda i: row_arrive(k, i))

    def both_arrivals(k):
        def arrive(i):
            line_arrive(k, i)
            row_arrive(k - 1, i - 1)

        for_range(1, lines, arrive)
        row_arrive(k - 1, lines - 1)

    def core_arrivals(k, x):
        for_range(0, lines, lambda i: core_copy(k, x, i).wait_recv())

    pl.semaphore_wait(barrier, lines + 2)
    for k in range(2):
        line_sends(k)
        own_sends(k)

    amp_load.wait()
    for x in range(ROW):
        for c in range(CORES):

            def fill(i, x=x, c=c):
                source = blk_of(
                    (line + i) % lines,
                    (row + x) % ROW,
                    (core + c) % CORES,
                )
                tiles = []
                for m in range(most):
                    task = tasks_ref[m, 0, source]
                    local = owner_ref[jnp.maximum(task, 0)] - me * hold
                    tiles.append(jnp.where(task >= 0, local, -1))
                at = pl.multiple_of(((x * lines + i) * CORES + c) * depth, depth)
                for h in range(hold):
                    slot = jnp.int32(0)
                    live = jnp.int32(0)
                    for m in range(most):
                        hit = tiles[m] == h
                        slot = jnp.where(hit, m, slot)
                        live = jnp.where(hit, 1, live)
                    tile = amp_ref[source, slot]
                    dense[h * rows : (h + 1) * rows, pl.ds(at, depth)] = jnp.where(
                        live > 0, tile, jnp.zeros_like(tile)
                    )

            for_range(0, lines, fill)

    span = lines * CORES * depth

    def product(k, x):
        width = min(span, 2048)

        def term(j):
            first = pl.multiple_of(j * width, width)
            block = slabs[k, x, pl.ds(j * (width // (CORES * depth)), width // (CORES * depth))]
            return jnp.dot(
                dense[:, pl.ds(x * span + first, width)],
                block.reshape(width, LANES),
                preferred_element_type=jnp.float32,
            )

        if span == width:
            return term(0)
        zero = jnp.zeros((hold * rows, LANES), jnp.float32)
        return lax.fori_loop(0, span // width, lambda j, total: total + term(j), zero)

    def near(k):
        core_arrivals(k, 0)
        if k < chunks:
            outgoing[k] = product(k, 0)
        else:
            keep_ref[:, pl.ds((k - chunks) * LANES, LANES)] = product(k, 0)

    def far(k):
        core_arrivals(k, 1)
        if k < chunks:
            outgoing[k] += product(k, 1)
            for h in range(hold):
                sum_copy(k, h).start()
        else:
            keep_ref[:, pl.ds((k - chunks) * LANES, LANES)] += product(k, 1)

    line_arrivals(0)
    for k in range(1, steps):
        if k + 1 < steps:
            line_sends(k + 1)
            own_sends(k + 1)
        both_arrivals(k)
        if k - 1 < chunks:
            near(k - 1)
            far(k - 1)
    row_arrivals(steps - 1)
    for k in range(chunks, steps):
        near(k)
        far(k)

    for k in range(chunks):
        for h in range(hold):
            sum_copy(k, h).wait()
    for k in range(steps):
        for_range(1, lines, lambda i: line_copy(k, i).wait_send())

        def sent(i):
            row_copy(k, i).wait_send()
            for x in range(ROW):
                core_copy(k, x, i).wait_send()

        for_range(0, lines, sent)


def per_device(mesh, amplitudes, integral_slabs, tile_tasks, owner_map):
    amp = amplitudes[0, 0]
    slab = integral_slabs[0]
    count, most, rows, depth = amp.shape
    devices, groups = mesh.shape["blk"], mesh.shape["grp"]
    hold = owner_map.shape[0] // devices
    columns = slab.shape[1]
    half = columns // groups
    lines = devices // (ROW * CORES)
    chunks = half // LANES
    steps = groups * chunks
    dma = pltpu.SemaphoreType.DMA
    total = jax.ShapeDtypeStruct((hold * rows, half), jnp.float32)
    keep, recv = pl.pallas_call(
        functools.partial(kernel, (lines, hold, most, rows, depth, half)),
        out_shape=(total, total),
        in_specs=[
            pl.BlockSpec(memory_space=pltpu.SMEM),
            pl.BlockSpec(memory_space=pltpu.SMEM),
            pl.BlockSpec(memory_space=pl.ANY),
            pl.BlockSpec(memory_space=pl.ANY),
        ],
        out_specs=(
            pl.BlockSpec(memory_space=pltpu.VMEM),
            pl.BlockSpec(memory_space=pltpu.VMEM),
        ),
        scratch_shapes=[
            pltpu.VMEM(amp.shape, amp.dtype),
            pltpu.VMEM((steps, ROW, lines, CORES, depth, LANES), slab.dtype),
            pltpu.VMEM((hold * rows, count * depth), amp.dtype),
            pltpu.VMEM((chunks, hold * rows, LANES), jnp.float32),
            dma,
            dma((steps,)),
            dma((steps, lines)),
            dma((steps, lines)),
            dma((steps, lines)),
            dma((steps, lines)),
            dma((steps, ROW, lines)),
            dma((steps, ROW, lines)),
            dma((chunks, hold)),
            dma((chunks, hold)),
        ],
        compiler_params=pltpu.CompilerParams(
            collective_id=0, has_side_effects=True, vmem_limit_bytes=60 * 1024 * 1024
        ),
    )(tile_tasks[0].transpose(2, 0, 1), owner_map, amp, slab)
    return keep + recv


def solution(mesh):
    placed = (
        P("blk", "grp", None, None, None, None),
        P("grp", "blk", None),
        P("blk", "grp", None, None),
        P(),
    )
    return jax.shard_map(
        functools.partial(per_device, mesh),
        mesh=mesh,
        in_specs=placed,
        out_specs=P("blk", "grp"),
        check_vma=False,
    )
```

```python
import functools

import jax
import jax.numpy as jnp
from jax import lax
from jax.experimental import pallas as pl
from jax.experimental.pallas import tpu as pltpu
from jax.sharding import PartitionSpec as P

MESH = pl.DeviceIdType.MESH
LANES = 128
ROW = 2
CORES = 2


def for_range(low, high, body):
    if high - low <= 8:
        for i in range(low, high):
            body(i)
    else:
        pl.loop(low, high)(body)


def kernel(
    dims,
    tasks_ref,
    owner_ref,
    amp_hbm,
    slab_hbm,
    keep_ref,
    recv_ref,
    amp_ref,
    slabs,
    dense,
    outgoing,
    amp_sem,
    slab_sem,
    line_send,
    line_recv,
    row_send,
    row_recv,
    core_send,
    core_recv,
    sum_send,
    sum_recv,
):
    lines, hold, most, rows, depth, half = dims
    chunks = half // LANES
    steps = 2 * chunks
    me = lax.axis_index("blk")
    grp = lax.axis_index("grp")
    core = me % CORES
    row = (me // CORES) % ROW
    line = me // (CORES * ROW)

    def blk_of(z, x, c):
        return (z * ROW + x) * CORES + c

    def line_peer(i):
        return blk_of((line + i) % lines, row, core)

    row_peer = blk_of(line, 1 - row, core)
    core_peer = blk_of(line, row, 1 - core)

    def column(k):
        side = 1 - grp if k < chunks else grp
        return pl.multiple_of(side * half + (k % chunks) * LANES, LANES)

    loads = [
        pltpu.make_async_copy(
            slab_hbm.at[:, pl.ds(column(k), LANES)], slabs.at[k, 0, 0, 0], slab_sem.at[k]
        )
        for k in range(steps)
    ]
    for load in loads:
        load.start()
    amp_load = pltpu.make_async_copy(amp_hbm, amp_ref, amp_sem)
    amp_load.start()

    barrier = pltpu.get_barrier_semaphore()

    def greet(blk, g):
        pl.semaphore_signal(barrier, inc=1, device_id=(blk, g), device_id_type=MESH)

    for_range(1, lines, lambda i: greet(line_peer(i), grp))
    greet(row_peer, grp)
    greet(core_peer, grp)
    greet(me, 1 - grp)

    def line_copy(k, i):
        return pltpu.make_async_remote_copy(
            src_ref=slabs.at[k, 0, 0, 0],
            dst_ref=slabs.at[k, 0, i, 0],
            send_sem=line_send.at[k, i],
            recv_sem=line_recv.at[k, i],
            device_id=(line_peer(lines - i), grp),
            device_id_type=MESH,
        )

    def row_copy(k, i):
        return pltpu.make_async_remote_copy(
            src_ref=slabs.at[k, 0, i, 0],
            dst_ref=slabs.at[k, 1, i, 0],
            send_sem=row_send.at[k, i],
            recv_sem=row_recv.at[k, i],
            device_id=(row_peer, grp),
            device_id_type=MESH,
        )

    def core_copy(k, x, i):
        return pltpu.make_async_remote_copy(
            src_ref=slabs.at[k, x, i, 0],
            dst_ref=slabs.at[k, x, i, 1],
            send_sem=core_send.at[k, x, i],
            recv_sem=core_recv.at[k, x, i],
            device_id=(core_peer, grp),
            device_id_type=MESH,
        )

    def sum_copy(k, h):
        at = pl.ds(h * rows, rows)
        return pltpu.make_async_remote_copy(
            src_ref=outgoing.at[k, at],
            dst_ref=recv_ref.at[at, pl.ds(k * LANES, LANES)],
            send_sem=sum_send.at[k, h],
            recv_sem=sum_recv.at[k, h],
            device_id=(me, 1 - grp),
            device_id_type=MESH,
        )

    def line_sends(k):
        loads[k].wait()
        for_range(1, lines, lambda i: line_copy(k, lines - i).start())

    def own_sends(k):
        row_copy(k, 0).start()
        core_copy(k, 0, 0).start()

    def line_arrive(k, i):
        line_copy(k, i).wait_recv()
        row_copy(k, i).start()
        core_copy(k, 0, i).start()

    def row_arrive(k, i):
        row_copy(k, i).wait_recv()
        core_copy(k, 1, i).start()

    def line_arrivals(k):
        for_range(1, lines, lambda i: line_arrive(k, i))

    def row_arrivals(k):
        for_range(0, lines, lambda i: row_arrive(k, i))

    def both_arrivals(k):
        def arrive(i):
            line_arrive(k, i)
            row_arrive(k - 1, i - 1)

        for_range(1, lines, arrive)
        row_arrive(k - 1, lines - 1)

    def core_arrivals(k, x):
        for_range(0, lines, lambda i: core_copy(k, x, i).wait_recv())

    pl.semaphore_wait(barrier, lines + 2)
    for k in range(2):
        line_sends(k)
        own_sends(k)

    amp_load.wait()
    for x in range(ROW):
        for c in range(CORES):

            def fill(i, x=x, c=c):
                source = blk_of(
                    (line + i) % lines,
                    (row + x) % ROW,
                    (core + c) % CORES,
                )
                tiles = []
                for m in range(most):
                    task = tasks_ref[m, 0, source]
                    local = owner_ref[jnp.maximum(task, 0)] - me * hold
                    tiles.append(jnp.where(task >= 0, local, -1))
                at = pl.multiple_of(((x * lines + i) * CORES + c) * depth, depth)
                for h in range(hold):
                    slot = jnp.int32(0)
                    live = jnp.int32(0)
                    for m in range(most):
                        hit = tiles[m] == h
                        slot = jnp.where(hit, m, slot)
                        live = jnp.where(hit, 1, live)
                    tile = amp_ref[source, slot]
                    dense[h * rows : (h + 1) * rows, pl.ds(at, depth)] = jnp.where(
                        live > 0, tile, jnp.zeros_like(tile)
                    )

            for_range(0, lines, fill)

    span = lines * CORES * depth

    def product(k, x):
        width = min(span, 2048)

        def term(j):
            first = pl.multiple_of(j * width, width)
            block = slabs[k, x, pl.ds(j * (width // (CORES * depth)), width // (CORES * depth))]
            return jnp.dot(
                dense[:, pl.ds(x * span + first, width)],
                block.reshape(width, LANES),
                preferred_element_type=jnp.float32,
            )

        if span == width:
            return term(0)
        zero = jnp.zeros((hold * rows, LANES), jnp.float32)
        return lax.fori_loop(0, span // width, lambda j, total: total + term(j), zero)

    def near(k):
        core_arrivals(k, 0)
        if k < chunks:
            outgoing[k] = product(k, 0)
        else:
            keep_ref[:, pl.ds((k - chunks) * LANES, LANES)] = product(k, 0)

    def far(k):
        core_arrivals(k, 1)
        if k < chunks:
            outgoing[k] += product(k, 1)
            for h in range(hold):
                sum_copy(k, h).start()
        else:
            keep_ref[:, pl.ds((k - chunks) * LANES, LANES)] += product(k, 1)

    line_arrivals(0)
    for k in range(1, steps):
        if k + 1 < steps:
            line_sends(k + 1)
            own_sends(k + 1)
        both_arrivals(k)
        if k - 1 < chunks:
            near(k - 1)
            far(k - 1)
    row_arrivals(steps - 1)
    for k in range(chunks, steps):
        near(k)
        far(k)

    for k in range(chunks):
        for h in range(hold):
            sum_copy(k, h).wait()
            at = pl.ds(h * rows, rows)
            lanes = pl.ds(k * LANES, LANES)
            keep_ref[at, lanes] += recv_ref[at, lanes]
    for k in range(steps):
        for_range(1, lines, lambda i: line_copy(k, i).wait_send())

        def sent(i):
            row_copy(k, i).wait_send()
            for x in range(ROW):
                core_copy(k, x, i).wait_send()

        for_range(0, lines, sent)


def per_device(mesh, amplitudes, integral_slabs, tile_tasks, owner_map):
    amp = amplitudes[0, 0]
    slab = integral_slabs[0]
    count, most, rows, depth = amp.shape
    devices, groups = mesh.shape["blk"], mesh.shape["grp"]
    hold = owner_map.shape[0] // devices
    columns = slab.shape[1]
    half = columns // groups
    lines = devices // (ROW * CORES)
    chunks = half // LANES
    steps = groups * chunks
    dma = pltpu.SemaphoreType.DMA
    total = jax.ShapeDtypeStruct((hold * rows, half), jnp.float32)
    return pl.pallas_call(
        functools.partial(kernel, (lines, hold, most, rows, depth, half)),
        out_shape=total,
        in_specs=[
            pl.BlockSpec(memory_space=pltpu.SMEM),
            pl.BlockSpec(memory_space=pltpu.SMEM),
            pl.BlockSpec(memory_space=pl.ANY),
            pl.BlockSpec(memory_space=pl.ANY),
        ],
        out_specs=pl.BlockSpec(memory_space=pltpu.VMEM),
        scratch_shapes=[
            pltpu.VMEM((hold * rows, half), jnp.float32),
            pltpu.VMEM(amp.shape, amp.dtype),
            pltpu.VMEM((steps, ROW, lines, CORES, depth, LANES), slab.dtype),
            pltpu.VMEM((hold * rows, count * depth), amp.dtype),
            pltpu.VMEM((chunks, hold * rows, LANES), jnp.float32),
            dma,
            dma((steps,)),
            dma((steps, lines)),
            dma((steps, lines)),
            dma((steps, lines)),
            dma((steps, lines)),
            dma((steps, ROW, lines)),
            dma((steps, ROW, lines)),
            dma((chunks, hold)),
            dma((chunks, hold)),
        ],
        compiler_params=pltpu.CompilerParams(
            collective_id=0, has_side_effects=True, vmem_limit_bytes=60 * 1024 * 1024
        ),
    )(tile_tasks[0].transpose(2, 0, 1), owner_map, amp, slab)


def solution(mesh):
    placed = (
        P("blk", "grp", None, None, None, None),
        P("grp", "blk", None),
        P("blk", "grp", None, None),
        P(),
    )
    return jax.shard_map(
        functools.partial(per_device, mesh),
        mesh=mesh,
        in_specs=placed,
        out_specs=P("blk", "grp"),
        check_vma=False,
    )
```
